32 devices in a mesh: aa: 4 (over x, core), ba: 8 (over z, y).
Axes of the slice: x: 2, y: 2, z: 4, core: 2. Of those that a mesh axis runs over, the one named last changes fastest.
Arguments:
- initial_dictionary_matrix: bfloat16 [32768, 3584], P('ba', 'aa'), may hold values from -60 to 60
- decoder_two: bfloat16 [32768, 3584], P('ba', 'aa'), may hold values from -60 to 60
- route_one: int32 [8, 8], replicated, may hold values from 0 to 7
- route_two: int32 [8, 8], replicated, may hold values from 0 to 7
- candidate_pair_slots: int32 [8, 24, 2], P('ba'), may hold values from 0 to 7
Outputs:
- leading_logarithmic_factor: float32 [32768], P('ba')
- col_log_scale: float32 [32768], P('ba')
The draws below stay inside these ranges and needn't reach their ends.
All inputs are finite; a program needn't handle non-finite values.
Results may differ from the reference program's by a relative error of at most 0.00046.
Values may be sent and summed in bfloat16 or wider, within the bound.
A program may use at most 128 MiB of HBM per device.

```python
import math
import jax
import jax.numpy as jnp
from jax import lax

D = 3584
BS = 512
PAIRS_COL = 24
SWEEPS = 4
NF = 32768
BLK_DEV = 8
NBLK = 64
N_BA = 8


def draw_decoder(key, count, width):
    key_scale, key_body = jax.random.split(key, 2)
    scales = jnp.exp(jax.random.uniform(key_scale, (count, 1), jnp.float32, 0.0, math.log(10.0)))
    values = jnp.clip(jax.random.normal(key_body, (count, width), jnp.float32), -6.0, 6.0)
    return (scales * values).astype(jnp.bfloat16)


def pairing_plan(key):
    folded_result = jax.random.fold_in(key, 101)
    key_first, key_second, key_pairs = jax.random.split(folded_result, 3)
    route_one = jax.random.randint(key_first, (N_BA, N_BA), 0, BLK_DEV, jnp.int32)
    route_two = jax.random.randint(key_second, (N_BA, N_BA), 0, BLK_DEV, jnp.int32)
    candidate_pair_slots = jax.random.randint(key_pairs, (N_BA, PAIRS_COL, 2), 0, N_BA, jnp.int32)
    return (route_one, route_two, candidate_pair_slots)


def draw_route_one(key, part):
    return pairing_plan(key)[0]


def draw_route_two(key, part):
    return pairing_plan(key)[1]


def draw_candidate_pair_slots(key, part):
    return pairing_plan(key)[2]


def draw_initial_dictionary_matrix(key, part):
    return draw_decoder(jax.random.fold_in(key, 11), NF, D)


def draw_decoder_two(key, part):
    source_rows = draw_decoder(jax.random.fold_in(key, 11), NF, D).astype(jnp.float32)
    fresh_rows = draw_decoder(jax.random.fold_in(key, 23), NF, D).astype(jnp.float32)
    route_one, route_two, candidate_pair_slots = pairing_plan(key)
    owners = jnp.broadcast_to(jnp.arange(N_BA, dtype=jnp.int32)[:, None], (N_BA, PAIRS_COL))
    source_one = candidate_pair_slots[:, :, 0]
    source_two = candidate_pair_slots[:, :, 1]
    row_block = (source_one * BLK_DEV + route_one[source_one, owners]).reshape(-1).astype(jnp.int32)
    col_block = (source_two * BLK_DEV + route_two[source_two, owners]).reshape(-1).astype(jnp.int32)
    pair_count = row_block.shape[0]
    pair_index = jnp.arange(pair_count, dtype=jnp.int32)
    matches = col_block[None, :] == jnp.arange(NBLK, dtype=jnp.int32)[:, None]
    earliest = jnp.min(jnp.where(matches, pair_index[None, :], pair_count), axis=1)
    present = earliest < pair_count
    partner = row_block[jnp.minimum(earliest, pair_count - 1)]
    key_pick, key_place, key_intersection = jax.random.split(jax.random.fold_in(key, 37), 3)
    row_ids = jnp.arange(NF, dtype=jnp.int32)
    block_of = row_ids // BS
    chosen = jnp.logical_and(present[block_of], jax.random.uniform(key_pick, (NF,), jnp.float32) < 0.25)
    selected_entry_line = partner[block_of] * BS + jax.random.randint(key_place, (NF,), 0, BS, jnp.int32)
    intersection = jax.random.uniform(key_intersection, (NF, 1), jnp.float32, 0.5, 0.95)
    target = source_rows[selected_entry_line]
    target = target / jnp.sqrt(jnp.sum(target * target, axis=1, keepdims=True) + 1e-12)
    projection = jnp.sum(fresh_rows * target, axis=1, keepdims=True)
    across = fresh_rows - projection * target
    length = jnp.sqrt(jnp.sum(fresh_rows * fresh_rows, axis=1, keepdims=True))
    across = across * (length / jnp.sqrt(jnp.sum(across * across, axis=1, keepdims=True) + 1e-12))
    planted_matching = intersection * length * target + jnp.sqrt(1.0 - intersection * intersection) * across
    values = jnp.where(chosen[:, None], planted_matching, fresh_rows)
    return jnp.clip(values, -60.0, 60.0).astype(jnp.bfloat16)


def setup_inputs(seed: int = 0) -> dict:
    key_list = jax.random.split(jax.random.key(seed), 6)
    return {
        "initial_dictionary_matrix": draw_initial_dictionary_matrix(jax.random.fold_in(key_list[5], 71), 0),
        "decoder_two": draw_decoder_two(jax.random.fold_in(key_list[5], 71), 0),
        "route_one": draw_route_one(jax.random.fold_in(key_list[5], 71), 0),
        "route_two": draw_route_two(jax.random.fold_in(key_list[5], 71), 0),
        "candidate_pair_slots": draw_candidate_pair_slots(jax.random.fold_in(key_list[5], 71), 0),
    }


smoothing_regularizer = 0.02
norm_floor = 1e-06

def unit_rows(decoder):
    widened = decoder.astype(jnp.float32)
    squares = lax.optimization_barrier(jnp.sum(widened * widened, axis=1, keepdims=True))
    return (widened * lax.rsqrt(squares + norm_floor)).astype(jnp.bfloat16)

def reference(initial_dictionary_matrix, decoder_two, route_one, route_two, candidate_pair_slots):
    unit_one = unit_rows(initial_dictionary_matrix).reshape(NBLK, BS, D)
    unit_two = unit_rows(decoder_two).reshape(NBLK, BS, D)
    owners = jnp.broadcast_to(jnp.arange(N_BA, dtype=jnp.int32)[:, None], (N_BA, PAIRS_COL))
    source_one = candidate_pair_slots[:, :, 0]
    source_two = candidate_pair_slots[:, :, 1]
    row_block = (source_one * BLK_DEV + route_one[source_one, owners]).reshape(-1).astype(jnp.int32)
    col_block = (source_two * BLK_DEV + route_two[source_two, owners]).reshape(-1).astype(jnp.int32)

    def kernel_of(blocks):
        angular_agreement = jnp.dot(unit_one[blocks[0]], unit_two[blocks[1]].T, preferred_element_type=jnp.float32)
        return jnp.exp(angular_agreement / smoothing_regularizer)
    exponential_affinity = lax.map(kernel_of, (row_block, col_block))
    col_scale = jnp.ones((NBLK, BS), jnp.float32)
    row_scale = jnp.ones((NBLK, BS), jnp.float32)
    for sweep_index in range(SWEEPS):
        row_terms = jnp.einsum('pij,pj->pi', exponential_affinity, col_scale[col_block], precision=lax.Precision.HIGHEST)
        row_scale = 1.0 / (1.0 + jax.ops.segment_sum(row_terms, row_block, num_segments=NBLK))
        col_terms = jnp.einsum('pij,pi->pj', exponential_affinity, row_scale[row_block], precision=lax.Precision.HIGHEST)
        col_scale = 1.0 / (1.0 + jax.ops.segment_sum(col_terms, col_block, num_segments=NBLK))
    return (jnp.log(row_scale).reshape(NF), jnp.log(col_scale).reshape(NF))
```

```python
import functools

import jax
import jax.numpy as jnp
from jax import lax
from jax.experimental import pallas as pl
from jax.experimental.pallas import tpu as pltpu
from jax.sharding import PartitionSpec as P

BS = 512
SWEEPS = 4
MESH = pl.DeviceIdType.MESH

smoothing_regularizer = 0.02
norm_floor = 1e-06


def exchange(buf, send_sem, recv_sem, step, axis, me, n):
    copies = []
    for d in range(1, n):
        peer = lax.rem(me + d, n)
        copy = pltpu.make_async_remote_copy(
            src_ref=buf.at[step, me],
            dst_ref=buf.at[step, me],
            send_sem=send_sem.at[step, d],
            recv_sem=recv_sem.at[step, me],
            device_id={axis: peer},
            device_id_type=MESH,
        )
        copy.start()
        copies.append(copy)
    for d in range(1, n):
        source = lax.rem(me + n - d, n)
        pltpu.make_async_remote_copy(
            src_ref=buf.at[step, source],
            dst_ref=buf.at[step, source],
            send_sem=send_sem.at[step, d],
            recv_sem=recv_sem.at[step, source],
            device_id={axis: source},
            device_id_type=MESH,
        ).wait_recv()
    for copy in copies:
        copy.wait_send()


def sweeps_kernel(
    n_aa,
    n_ba,
    row_src,
    col_src,
    cosine,
    same_one,
    same_two,
    final_one,
    final_two,
    row_out,
    col_out,
    k_hi,
    k_lo,
    kt_hi,
    kt_lo,
    part,
    full,
    part_send,
    part_recv,
    full_send,
    full_recv,
):
    a = lax.axis_index("aa")
    b = lax.axis_index("ba")
    owned = cosine.shape[0]
    barrier = pltpu.get_barrier_semaphore()
    for d in range(1, n_aa):
        pl.semaphore_signal(barrier, inc=1, device_id={"aa": lax.rem(a + d, n_aa)}, device_id_type=MESH)
    for d in range(1, n_ba):
        pl.semaphore_signal(barrier, inc=1, device_id={"ba": lax.rem(b + d, n_ba)}, device_id_type=MESH)

    def prepare(q, carry):
        k = jnp.exp(cosine[q] * (1.0 / smoothing_regularizer))
        hi = k.astype(jnp.bfloat16)
        k_hi[q] = hi
        k_lo[q] = (k - hi.astype(jnp.float32)).astype(jnp.bfloat16)
        kt = k.T
        hi = kt.astype(jnp.bfloat16)
        kt_hi[q] = hi
        kt_lo[q] = (kt - hi.astype(jnp.float32)).astype(jnp.bfloat16)
        return carry

    lax.fori_loop(0, owned, prepare, 0)
    pl.semaphore_wait(barrier, n_aa - 1 + n_ba - 1)

    ids = lax.broadcasted_iota(jnp.int32, (n_ba, BS), 0)
    lane_rows = lax.broadcasted_iota(jnp.int32, (16, BS), 0)

    def half(step, scale, source, target, hi_ref, lo_ref, same):
        def one(q, acc):
            v = jnp.sum(jnp.where(ids == source[q], scale, 0.0), axis=0, keepdims=True)
            v_hi = v.astype(jnp.bfloat16).astype(jnp.float32)
            v_lo = v - v_hi
            lhs = jnp.where(
                lane_rows == 0,
                jnp.broadcast_to(v_hi, (16, BS)),
                jnp.where(lane_rows == 1, jnp.broadcast_to(v_lo, (16, BS)), 0.0),
            ).astype(jnp.bfloat16)
            got = jnp.dot(lhs, hi_ref[q], preferred_element_type=jnp.float32) + jnp.dot(
                lhs, lo_ref[q], preferred_element_type=jnp.float32
            )
            term = jnp.sum(got, axis=0, keepdims=True)
            return acc + jnp.where(ids == target[q], jnp.broadcast_to(term, (n_ba, BS)), 0.0)

        part[step, a] = lax.fori_loop(0, owned, one, jnp.zeros((n_ba, BS), jnp.float32))
        exchange(part, part_send, part_recv, step, "aa", a, n_aa)
        mine = part[step, 0]
        for i in range(1, n_aa):
            mine = mine + part[step, i]
        full[step, b] = mine
        exchange(full, full_send, full_recv, step, "ba", b, n_ba)
        total = jnp.zeros((n_ba, BS), jnp.float32)
        for i in range(n_ba):
            total = total + jnp.where(same[i] > 0.0, full[step, i], 0.0)
        return 1.0 / (1.0 + total)

    def sweep(i, col_scale):
        row_scale = half(2 * i, col_scale, col_src, row_src, kt_hi, kt_lo, same_one)
        return half(2 * i + 1, row_scale, row_src, col_src, k_hi, k_lo, same_two)

    lax.fori_loop(0, SWEEPS, sweep, jnp.ones((n_ba, BS), jnp.float32))

    for step, final, out in ((2 * SWEEPS - 2, final_one, row_out), (2 * SWEEPS - 1, final_two, col_out)):
        total = jnp.zeros(out.shape, jnp.float32)
        for i in range(n_ba):
            row = full[step, i, pl.ds(b, 1), :]
            total = total + jnp.where(final[i] > 0.0, jnp.broadcast_to(row, out.shape), 0.0)
        out[...] = jnp.log(1.0 / (1.0 + total))


def balance(cosine, row_src, col_src, same_one, same_two, final_one, final_two, n_aa, n_ba, blocks_dev):
    owned = cosine.shape[0]
    vmem = pl.BlockSpec(memory_space=pltpu.VMEM)
    smem = pl.BlockSpec(memory_space=pltpu.SMEM)
    out = jax.ShapeDtypeStruct((blocks_dev, BS), jnp.float32)
    halves = pltpu.VMEM((owned, BS, BS), jnp.bfloat16)
    steps = 2 * SWEEPS
    return pl.pallas_call(
        functools.partial(sweeps_kernel, n_aa, n_ba),
        out_shape=(out, out),
        in_specs=[smem, smem] + [vmem] * 5,
        out_specs=(vmem, vmem),
        scratch_shapes=[
            halves,
            halves,
            halves,
            halves,
            pltpu.VMEM((steps, n_aa, n_ba, BS), jnp.float32),
            pltpu.VMEM((steps, n_ba, n_ba, BS), jnp.float32),
            pltpu.SemaphoreType.DMA((steps, n_aa)),
            pltpu.SemaphoreType.DMA((steps, n_aa)),
            pltpu.SemaphoreType.DMA((steps, n_ba)),
            pltpu.SemaphoreType.DMA((steps, n_ba)),
        ],
        compiler_params=pltpu.CompilerParams(collective_id=0, has_side_effects=True),
        name="sweeps",
    )(row_src, col_src, cosine, same_one, same_two, final_one, final_two)


def per_device(initial_dictionary_matrix, decoder_two, route_one, route_two, candidate_pair_slots):
    column = lax.axis_index("ba")
    depth = lax.axis_size("aa")
    depth_index = lax.axis_index("aa")
    owners = lax.axis_size("ba")
    width = initial_dictionary_matrix.shape[1]
    blocks_dev = initial_dictionary_matrix.shape[0] // BS
    sum_one = jnp.sum(jnp.square(initial_dictionary_matrix.astype(jnp.float32)), axis=1)
    sum_two = jnp.sum(jnp.square(decoder_two.astype(jnp.float32)), axis=1)
    sum_one, sum_two = lax.psum((sum_one, sum_two), "aa")
    unit_one = (
        initial_dictionary_matrix.astype(jnp.float32) * lax.rsqrt(sum_one + norm_floor)[:, None]
    ).astype(jnp.bfloat16)
    unit_two = (decoder_two.astype(jnp.float32) * lax.rsqrt(sum_two + norm_floor)[:, None]).astype(
        jnp.bfloat16
    )
    send_one = jnp.take(unit_one.reshape(blocks_dev, BS, width), route_one[column], axis=0)
    send_two = jnp.take(unit_two.reshape(blocks_dev, BS, width), route_two[column], axis=0)
    got_one, got_two = (
        lax.all_to_all(send_one, "ba", split_axis=0, concat_axis=0, tiled=True),
        lax.all_to_all(send_two, "ba", split_axis=0, concat_axis=0, tiled=True),
    )
    column_pairs = candidate_pair_slots[0]
    whole_pairs = column_pairs.shape[0]
    owned = whole_pairs // depth
    left = jnp.take(got_one, column_pairs[:, 0], axis=0)
    right = jnp.take(got_two, column_pairs[:, 1], axis=0)
    cosine = lax.psum_scatter(
        jnp.einsum("qid,qjd->qij", left, right, preferred_element_type=jnp.float32),
        "aa",
        scatter_dimension=0,
        tiled=True,
    )
    my_pairs = lax.dynamic_slice_in_dim(column_pairs, depth_index * owned, owned, 0)

    def masks(route):
        same = (route == route[:, column][:, None]).T
        final = route[column][:, None] == jnp.arange(blocks_dev, dtype=jnp.int32)[None, :]
        return (
            jnp.broadcast_to(same.astype(jnp.float32)[:, :, None], (owners, owners, BS)),
            jnp.broadcast_to(final.astype(jnp.float32)[:, :, None], (owners, blocks_dev, BS)),
        )

    same_one, final_one = masks(route_one)
    same_two, final_two = masks(route_two)
    row_log, col_log = balance(
        cosine,
        my_pairs[:, 0],
        my_pairs[:, 1],
        same_one,
        same_two,
        final_one,
        final_two,
        depth,
        owners,
        blocks_dev,
    )
    return (row_log.reshape(-1), col_log.reshape(-1))


def solution(mesh):
    placed = (P("ba", "aa"), P("ba", "aa"), P(), P(), P("ba", None, None))
    return jax.shard_map(
        per_device, mesh=mesh, in_specs=placed, out_specs=(P("ba"), P("ba")), check_vma=False
    )
```
